128 devices in a mesh: ka: 4 (over x_hi, core), brick: 32 (over z, x_lo, y).
Axes of the slice: x: 4 (x_hi: 2, x_lo: 2; x = x_hi * 2 + x_lo), y: 4, z: 4, core: 2. Of those that a mesh axis runs over, the one named last changes fastest.
Arguments:
- spinors: bfloat16 [32, 4, 128, 36864], P('ka', None, 'brick'), may hold values from -6 to 6
- kpt_mult: int32 [32], P('ka'), may hold values from 1 to 4
- occupied: int32 [32], P('ka'), may hold values 0 or 1
- core_density: float32 [128, 36864], P('brick'), may hold values from 0.05 to 1
- local_potential: float32 [128, 36864], P('brick'), may hold values from -6 to 6
Outputs:
- applied: bfloat16 [32, 4, 128, 36864], P('ka', None, 'brick')
The draws below stay inside these ranges and needn't reach their ends.
All inputs are finite; a program needn't handle non-finite values. No bound on the sum of `occupied` on one device may be relied on, other than what follows from the above.
Results may differ from the reference program's by a relative error of at most 0.005.
Values may be sent and summed in bfloat16 or wider, within the bound.
A program may use at most 128 MiB of HBM per device.

```python
import math
import jax
import jax.numpy as jnp
from jax import lax

NY = 192
CELLS = 36864
B_TOTAL = 32
NZ = 128


def plant(values, key, least, high):
    longest = values.shape.index(max(values.shape))
    spots = []
    for shift in (0, 1):
        where = [jax.random.randint(jax.random.fold_in(key, axis), (), 0, length) for axis, length in enumerate(values.shape)]
        where[longest] = (where[longest] + shift) % values.shape[longest]
        spots.append(tuple(where))
    return values.at[spots[0]].set(least).at[spots[1]].set(high)


def level_of(rng, extent, pieces, least, high):
    gain, own = 1.0, jax.random.fold_in(rng, 6)
    for position, shards_of in pieces:
        draws = jnp.exp(jax.random.uniform(jax.random.fold_in(own, position), (shards_of,), jnp.float32, least / len(pieces), high / len(pieces)))
        gain = gain * jnp.repeat(draws, extent[position] // shards_of).reshape([-1 if axis == position else 1 for axis in range(len(extent))])
    return gain


def scatter_about(own_key, dims, spread, bound, pieces=(), held_as=jnp.bfloat16):
    level = level_of(own_key, dims, pieces, -0.22, 0.18) if pieces else 1.0
    values = jax.random.normal(own_key, dims, jnp.float32) * spread * level
    return jnp.minimum(jnp.maximum(values, -bound), bound).astype(held_as)


def setup_inputs(seed: int = 0) -> dict:
    keys = jax.random.split(jax.random.key(seed), 6)
    spinors = scatter_about(keys[0], (B_TOTAL, 4, NZ, CELLS), 1.0, 6.0, ((0, 4), (2, 32)))
    kpt_mult = plant(jax.random.randint(keys[1], (B_TOTAL,), 1, 5), jax.random.fold_in(keys[1], 1), 1, 4).astype(jnp.int32)
    occupied = plant((jax.random.randint(keys[2], (B_TOTAL,), 0, 4) < 3).astype(jnp.int32), jax.random.fold_in(keys[2], 1), 0, 1)
    core_density = jnp.clip(jnp.exp(math.log(1.0) - 2.9957323 * jax.random.uniform(keys[3], (NZ, CELLS), jnp.float32) ** level_of(keys[3], (NZ, CELLS), ((0, 32),), -0.2, 0.2)), 0.05, 1.0)
    local_potential = scatter_about(keys[4], (NZ, CELLS), 1.0, 6.0, ((0, 32),), jnp.float32)
    return {"spinors": spinors, "kpt_mult": kpt_mult, "occupied": occupied, "core_density": core_density, "local_potential": local_potential}


FLOOR_FRACTION = 0.05

def density_terms(band, weight):
    values = band.astype(jnp.float32)
    up_real, up_imag, down_real, down_imag = (values[0], values[1], values[2], values[3])
    up_square = up_real * up_real + up_imag * up_imag
    down_square = down_real * down_real + down_imag * down_imag
    return weight * jnp.stack([up_square + down_square, 2.0 * (up_real * down_real + up_imag * down_imag), 2.0 * (up_real * down_imag - up_imag * down_real), up_square - down_square])

def accumulate_density(spinors, weights):
    zeros = jnp.zeros((4,) + spinors.shape[2:], jnp.float32)

    def step_band(carry, item):
        band, weight = item
        return (carry + density_terms(band, weight), None)
    result, unused = lax.scan(step_band, zeros, (spinors, weights))
    return result

def frame_potential(density, core):
    electrons = density[0] + core
    magnitude = jnp.sqrt(density[1] * density[1] + density[2] * density[2] + density[3] * density[3])
    upper = -jnp.cbrt(3.0 / math.pi * (electrons + magnitude))
    lower = -jnp.cbrt(3.0 / math.pi * (electrons - magnitude))
    factor = 0.5 * (upper - lower) / jnp.maximum(magnitude, FLOOR_FRACTION * electrons)
    return jnp.stack([0.5 * (upper + lower), factor * density[1], factor * density[2], factor * density[3]])

def plane_neighbours(center, row_length):
    column = jnp.arange(center.shape[-1], dtype=jnp.int32) % row_length
    forward = jnp.where(column == row_length - 1, jnp.roll(center, row_length - 1, -1), jnp.roll(center, -1, -1))
    backward = jnp.where(column == 0, jnp.roll(center, 1 - row_length, -1), jnp.roll(center, 1, -1))
    across = jnp.roll(center, row_length, -1) + jnp.roll(center, -row_length, -1)
    return forward + backward + across

def apply_hamiltonian(padded_band, potential):
    values = padded_band.astype(jnp.float32)
    center = values[:, 1:-1]
    neighbours = values[:, 2:] + values[:, :-2]
    neighbours = neighbours + plane_neighbours(center, NY)
    kinetic = -0.5 * (neighbours - 6.0 * center)
    diagonal_up = potential[0] + potential[3]
    diagonal_down = potential[0] - potential[3]
    field_x, field_y = (potential[1], potential[2])
    up_real, up_imag, down_real, down_imag = (center[0], center[1], center[2], center[3])
    mixed = jnp.stack([diagonal_up * up_real + field_x * down_real + field_y * down_imag, diagonal_up * up_imag + field_x * down_imag - field_y * down_real, field_x * up_real - field_y * up_imag + diagonal_down * down_real, field_x * up_imag + field_y * up_real + diagonal_down * down_imag])
    return (kinetic + mixed).astype(jnp.bfloat16)

def reference(spinors, kpt_mult, occupied, core_density, local_potential):
    weights = (kpt_mult * occupied).astype(jnp.float32) / (2.0 * B_TOTAL)
    density = accumulate_density(spinors, weights)
    potential = frame_potential(density, core_density)
    potential = jnp.concatenate([(potential[0] + local_potential)[None], potential[1:]], axis=0)

    def one_band(band):
        padded = jnp.pad(band, ((0, 0), (1, 1), (0, 0)))
        return apply_hamiltonian(padded, potential)
    return lax.map(one_band, spinors)
```

```python
import functools
import math

import jax
import jax.numpy as jnp
from jax import lax
from jax.experimental import pallas as pl
from jax.experimental.pallas import tpu as pltpu
from jax.sharding import PartitionSpec as P

NY = 192
FLOOR_FRACTION = 0.05
MESH = pl.DeviceIdType.MESH
LANES = 128
ROWS_PER_STEP = 16
LAST_PIECES = 4
DENSITY_PIECES = 4
EARLY = 2


def cube_root(x):
    root = jnp.exp(jnp.log(jnp.abs(x)) * (1.0 / 3.0))
    return jnp.where(x == 0.0, 0.0, jnp.where(x < 0.0, -root, root))


def halo_kernel(
    bands,
    tiles,
    kpt_ref,
    occ_ref,
    x_hbm,
    core_ref,
    local_ref,
    out_ref,
    xb,
    send_up,
    send_down,
    from_below,
    from_above,
    partial_,
    stage,
    stencil,
    own_density,
    partner_half,
    chip_half,
    opposite_half,
    relay,
    total_density,
    potential,
    load_sem,
    wrap_sem,
    up_send,
    up_recv,
    down_send,
    down_recv,
    pair_send,
    pair_recv,
    cross_send,
    cross_recv,
    relay_recv,
    relay_send,
    gather_send,
    gather_recv,
):
    ka, brick = lax.axis_index("ka"), lax.axis_index("brick")
    bricks = lax.axis_size("brick")
    groups = lax.axis_size("ka")
    side = lax.rem(ka, 2)
    has_above, has_below = brick < bricks - 1, brick > 0
    above = (ka, jnp.minimum(brick + 1, bricks - 1))
    below = (ka, jnp.maximum(brick - 1, 0))
    partner = (ka + 1 - 2 * side, brick)
    far = lax.rem(ka + 2, groups)
    opposite = (far, brick)
    mate = brick + 1 - 2 * lax.rem(brick, 2)
    row = lax.rem(brick, 4)
    edge = jnp.logical_or(row == 0, row == 3)
    inner = jnp.logical_not(edge)
    half = tiles // 2
    piece = half // DENSITY_PIECES
    direct = DENSITY_PIECES // 2

    barrier = pltpu.get_barrier_semaphore()

    @pl.when(has_above)
    def _():
        pl.semaphore_signal(barrier, inc=1, device_id=above, device_id_type=MESH)

    @pl.when(has_below)
    def _():
        pl.semaphore_signal(barrier, inc=1, device_id=below, device_id_type=MESH)

    for other in (partner, opposite, (far, mate)):
        pl.semaphore_signal(barrier, inc=1, device_id=other, device_id_type=MESH)

    def load(b, c):
        return pltpu.make_async_copy(
            x_hbm.at[b, c], xb.at[b, pl.ds(2, tiles), c], load_sem.at[b, c]
        )

    def wrap(end, c):
        source = tiles - 2 if end == 0 else 0
        target = 0 if end == 0 else tiles + 2
        return pltpu.make_async_copy(
            x_hbm.at[:, c, pl.ds(source, 2)],
            xb.at[:, pl.ds(target, 2), c],
            wrap_sem.at[end, c],
        )

    for b in range(bands):
        for c in range(4):
            load(b, c).start()
    for end in range(2):
        for c in range(4):
            wrap(end, c).start()

    last = bands - 1
    rows = 4 * tiles
    last_rows = rows // LAST_PIECES

    def slots(b):
        if b < last:
            return [(b, pl.ds(0, rows), b)]
        return [(b, pl.ds(k * last_rows, last_rows), last + k) for k in range(LAST_PIECES)]

    def up_copy(slot):
        b, r, s = slot
        return pltpu.make_async_remote_copy(
            send_up.at[b, r], from_below.at[b, r], up_send.at[s], up_recv.at[s],
            device_id=above, device_id_type=MESH,
        )

    def down_copy(slot):
        b, r, s = slot
        return pltpu.make_async_remote_copy(
            send_down.at[b, r], from_above.at[b, r], down_send.at[s], down_recv.at[s],
            device_id=below, device_id_type=MESH,
        )

    def extract(b):
        for c in range(4):
            load(b, c).wait()
        n = ROWS_PER_STEP

        def step(i, carry):
            j = i * n
            values = xb[b, pl.ds(2 + j, n)].reshape(n * 16, LANES)
            stage[...] = values.astype(jnp.float32)
            r = pl.multiple_of(4 * j, 4 * n)
            send_up[b, pl.ds(r, 4 * n)] = stage[pl.ds(3, 4 * n, stride=4)].astype(jnp.bfloat16)
            send_down[b, pl.ds(r, 4 * n)] = stage[pl.ds(0, 4 * n, stride=4)].astype(jnp.bfloat16)
            return carry

        lax.fori_loop(0, tiles // n, step, 0)

    def send(b):
        for slot in slots(b):

            @pl.when(has_above)
            def _():
                up_copy(slot).start()

            @pl.when(has_below)
            def _():
                down_copy(slot).start()

    for b in range(EARLY + 1):
        extract(b)
    pl.semaphore_wait(
        barrier, 3 + has_above.astype(jnp.int32) + has_below.astype(jnp.int32)
    )
    for b in range(EARLY):
        send(b)
    for b in range(EARLY + 1, bands):
        extract(b)

    low = lax.broadcasted_iota(jnp.int32, (8, LANES), 0) < 4
    weights = [
        (kpt_ref[b] * occ_ref[b]).astype(jnp.float32) * (1.0 / (2.0 * bands * groups))
        for b in range(bands)
    ]

    def swap(v):
        return pltpu.roll(v, 4, 0)

    def density_step(j, carry):
        for q in range(2):
            jj = 2 * j + q
            a = bb = cc = dd = None
            for b in range(bands):
                t = xb[b, 2 + jj].reshape(16, LANES).astype(jnp.float32)
                u, w = t[:8], t[8:]
                uw, ww = u * weights[b], w * weights[b]
                terms = (uw * u, ww * w, uw * w, uw * swap(w))
                if b == 0:
                    a, bb, cc, dd = terms
                else:
                    a, bb, cc, dd = (x + y for x, y in zip((a, bb, cc, dd), terms))
            n, z = a + bb, a - bb
            dd = jnp.where(low, dd, -dd)
            n, z = n + swap(n), z + swap(z)
            mx, my = 2.0 * (cc + swap(cc)), 2.0 * (dd + swap(dd))
            first = jnp.where(low, n, mx)
            second = jnp.where(low, my, z)
            own_density[jj] = jnp.concatenate([first, second], axis=0).astype(jnp.bfloat16)
        return carry

    mine, theirs = half * side, half * (1 - side)
    lax.fori_loop(
        0, half // 2, lambda i, c: density_step(theirs // 2 + i, c), 0
    )
    pair = pltpu.make_async_remote_copy(
        own_density.at[pl.ds(theirs, half)], partner_half, pair_send, pair_recv,
        device_id=partner, device_id_type=MESH,
    )
    lax.fori_loop(0, half // 2, lambda i, c: density_step(mine // 2 + i, c), 0)
    pair.start()

    def weights_of(t):
        i = lax.broadcasted_iota(jnp.int32, (6 * LANES, 2 * LANES), 0) + 2 * LANES * (t - 1)
        o = lax.broadcasted_iota(jnp.int32, (6 * LANES, 2 * LANES), 1) + 2 * LANES * t
        diff = i - o
        y = o - jnp.where(o >= NY, NY, 0) - jnp.where(o >= 2 * NY, NY, 0) - jnp.where(o >= 3 * NY, NY, 0)
        forward = jnp.where(y == NY - 1, 1 - NY, 1)
        backward = jnp.where(y == 0, NY - 1, -1)
        near = jnp.where(diff == forward, -0.5, 0.0) + jnp.where(diff == backward, -0.5, 0.0)
        across = jnp.where(diff == NY, -0.5, 0.0) + jnp.where(diff == -NY, -0.5, 0.0)
        return (near + across + jnp.where(diff == 0, 3.0, 0.0)).astype(jnp.bfloat16)

    for t in range(3):
        stencil[t] = weights_of(t)

    pair.wait()

    def cross_copy(k):
        return pltpu.make_async_remote_copy(
            chip_half.at[pl.ds(k * piece, piece)], opposite_half.at[pl.ds(k * piece, piece)],
            cross_send.at[k], cross_recv.at[k], device_id=opposite, device_id_type=MESH,
        )

    def first_leg(k):
        return pltpu.make_async_remote_copy(
            chip_half.at[pl.ds(k * piece, piece)], relay.at[k - direct],
            cross_send.at[k], relay_recv.at[k - direct],
            device_id=(ka, mate), device_id_type=MESH,
        )

    def second_leg(k):
        return pltpu.make_async_remote_copy(
            relay.at[k - direct], opposite_half.at[pl.ds(k * piece, piece)],
            relay_send.at[k - direct], cross_recv.at[k],
            device_id=(far, mate), device_id_type=MESH,
        )

    def sum_half(i, carry):
        a = own_density[mine + i].astype(jnp.float32)
        chip_half[i] = (a + partner_half[i].astype(jnp.float32)).astype(jnp.bfloat16)
        return carry

    def cross_start(k):
        if k < direct:
            cross_copy(k).start()
        else:

            @pl.when(edge)
            def _():
                first_leg(k).start()

            @pl.when(inner)
            def _():
                cross_copy(k).start()

    order = list(range(direct, DENSITY_PIECES)) + list(range(direct))
    for n, k in enumerate(order):
        lax.fori_loop(k * piece, (k + 1) * piece, sum_half, 0)
        if n:
            cross_start(order[n - 1])
    send(EARLY)
    cross_start(order[-1])
    for b in range(EARLY + 1, bands):
        send(b)

    for end in range(2):
        for c in range(4):
            wrap(end, c).wait()

    @pl.when(jnp.logical_not(has_below))
    def _():
        from_below[...] = jnp.zeros_like(from_below)

    @pl.when(jnp.logical_not(has_above))
    def _():
        from_above[...] = jnp.zeros_like(from_above)

    for k in range(direct, DENSITY_PIECES):

        @pl.when(inner)
        def _():
            first_leg(k).wait_recv()
            second_leg(k).start()

    def sum_total(i, carry):
        a = chip_half[i].astype(jnp.float32)
        total_density[mine + i] = (a + opposite_half[i].astype(jnp.float32)).astype(jnp.bfloat16)
        return carry

    def gather(k):
        r = pl.ds(mine + k * piece, piece)
        return pltpu.make_async_remote_copy(
            total_density.at[r], total_density.at[r], gather_send.at[k], gather_recv.at[k],
            device_id=partner, device_id_type=MESH,
        )

    order = list(range(DENSITY_PIECES))
    for k in order:
        cross_copy(k).wait_recv()
        lax.fori_loop(k * piece, (k + 1) * piece, sum_total, 0)
        if k:
            gather(k - 1).start()

    def potential_step(j, carry):
        t = total_density[j].astype(jnp.float32)
        first, second = t[:8], t[8:]
        other_first, other_second = swap(first), swap(second)
        n = jnp.where(low, first, other_first)
        mx = jnp.where(low, other_first, first)
        my = jnp.where(low, second, other_second)
        z = jnp.where(low, other_second, second)
        core = core_ref[j]
        local = local_ref[j]
        electrons = n + jnp.concatenate([core, core], axis=0)
        magnitude = jnp.sqrt(mx * mx + my * my + z * z)
        upper = -cube_root(3.0 / math.pi * (electrons + magnitude))
        lower = -cube_root(3.0 / math.pi * (electrons - magnitude))
        factor = 0.5 * (upper - lower) / jnp.maximum(magnitude, FLOOR_FRACTION * electrons)
        v = 0.5 * (upper + lower) + jnp.concatenate([local, local], axis=0)
        bz, by = factor * z, factor * my
        potential[j, 0] = v + bz
        potential[j, 1] = v - bz
        potential[j, 2] = factor * mx
        potential[j, 3] = jnp.where(low, by, -by)
        return carry

    lax.fori_loop(mine, mine + (DENSITY_PIECES - 1) * piece, potential_step, 0)
    gather(DENSITY_PIECES - 1).start()
    lax.fori_loop(mine + (DENSITY_PIECES - 1) * piece, mine + half, potential_step, 0)

    def gathered(k):
        r = pl.ds(theirs + k * piece, piece)
        return pltpu.make_async_remote_copy(
            total_density.at[r], total_density.at[r], gather_send.at[k], gather_recv.at[k],
            device_id=partner, device_id_type=MESH,
        )

    for k in range(DENSITY_PIECES):
        gathered(k).wait_recv()
        lax.fori_loop(theirs + k * piece, theirs + (k + 1) * piece, potential_step, 0)

    plane = lax.rem(lax.broadcasted_iota(jnp.int32, (8, LANES), 0), 4)
    lower_edge, upper_edge = plane == 0, plane == 3

    def normal(v):
        down = jnp.where(lower_edge, 0.0, pltpu.roll(v, 1, 0))
        up = jnp.where(upper_edge, 0.0, pltpu.roll(v, 7, 0))
        return -0.5 * (down + up)

    group = 8

    def apply(b, target):
        def step(i, carry):
            j0 = i * (6 * group)
            values = xb[b, pl.ds(j0, 6 * group + 4)].reshape(6 * group + 4, 16, LANES)
            for t in range(3):
                left = jnp.concatenate(
                    [
                        jnp.concatenate(
                            [values[6 * g + 2 * t + q] for g in range(group)], axis=0
                        )
                        for q in range(6)
                    ],
                    axis=1,
                )
                product = jnp.dot(left, stencil[t], preferred_element_type=jnp.float32)
                for g in range(group):
                    for e in range(2):
                        k = 6 * g + 2 * t + e
                        j = j0 + k
                        x = values[k + 2].astype(jnp.float32)
                        u, w = x[:8], x[8:]
                        r = product[16 * g : 16 * g + 16, LANES * e : LANES * (e + 1)]
                        bx, by = potential[j, 2], potential[j, 3]
                        hu = r[:8] + normal(u) + potential[j, 0] * u + bx * w + by * swap(w)
                        hw = r[8:] + normal(w) + potential[j, 1] * w + bx * u - by * swap(u)
                        s = pl.multiple_of(16 * j, 16)
                        partial_[target, pl.ds(s, 8)] = hu
                        partial_[target, pl.ds(s + 8, 8)] = hw
            return carry

        lax.fori_loop(0, tiles // (6 * group), step, 0)

    def finish(b, source):
        n = ROWS_PER_STEP

        def step(i, carry):
            r = pl.multiple_of(4 * n * i, 4 * n)
            s = pl.multiple_of(16 * n * i, 16 * n)
            below_values = from_below[b, pl.ds(r, 4 * n)].astype(jnp.float32)
            above_values = from_above[b, pl.ds(r, 4 * n)].astype(jnp.float32)
            lows, highs = pl.ds(s, 4 * n, stride=4), pl.ds(s + 3, 4 * n, stride=4)
            view = partial_.at[source]
            view[lows] = view[lows] - 0.5 * below_values
            view[highs] = view[highs] - 0.5 * above_values
            done = view[pl.ds(s, 16 * n)].astype(jnp.bfloat16)
            out_ref[b, pl.ds(n * i, n)] = done.reshape(n, 4, 4, LANES)
            return carry

        per_slot = tiles // n // len(slots(b))
        rest = tiles // n - per_slot * len(slots(b))
        start = 0
        for m, slot in enumerate(slots(b)):

            @pl.when(has_below)
            def _():
                up_copy(slot).wait_recv()

            @pl.when(has_above)
            def _():
                down_copy(slot).wait_recv()

            stop = ((m + 1) * tiles // len(slots(b))) // n
            lax.fori_loop(start, stop, step, 0)
            start = stop

    apply(0, 0)
    for b in range(1, bands):
        apply(b, b % 2)
        finish(b - 1, (b - 1) % 2)

    pair_done = []
    for k in range(DENSITY_PIECES):
        cross_copy(k).wait_send()
        gather(k).wait_send()
    for k in range(direct, DENSITY_PIECES):

        @pl.when(inner)
        def _():
            second_leg(k).wait_send()

    for b in range(bands):
        for slot in slots(b):

            @pl.when(has_above)
            def _():
                up_copy(slot).wait_send()

            @pl.when(has_below)
            def _():
                down_copy(slot).wait_send()

    finish(last, last % 2)


def write_kernel(bands, in_ref, out_hbm, sem):
    copies = [
        pltpu.make_async_copy(in_ref.at[b, :, c], out_hbm.at[b, c], sem.at[b, c])
        for b in range(bands)
        for c in range(4)
    ]
    for copy in copies:
        copy.start()
    for copy in copies:
        copy.wait()


def shards(spinors, kpt_mult, occupied, core_density, local_potential):
    bands, parts, planes, cells = spinors.shape
    tiles = cells // LANES
    half = tiles // 2
    piece = half // DENSITY_PIECES
    relayed = DENSITY_PIECES - DENSITY_PIECES // 2
    copies = bands - 1 + LAST_PIECES
    bf16, f32 = jnp.bfloat16, jnp.float32
    view = spinors.reshape(bands, parts, planes, tiles, LANES).transpose(0, 1, 3, 2, 4)
    core = core_density.reshape(planes, tiles, LANES).transpose(1, 0, 2)
    local = local_potential.reshape(planes, tiles, LANES).transpose(1, 0, 2)
    dma = pltpu.SemaphoreType.DMA
    in_vmem = pl.BlockSpec(memory_space=pltpu.VMEM)
    in_smem = pl.BlockSpec(memory_space=pltpu.SMEM)
    anywhere = pl.BlockSpec(memory_space=pl.ANY)
    applied = pl.pallas_call(
        functools.partial(halo_kernel, bands, tiles),
        out_shape=pltpu.VMEM((bands, tiles, parts, planes, LANES), bf16),
        in_specs=[in_smem, in_smem, anywhere, in_vmem, in_vmem],
        out_specs=in_vmem,
        scratch_shapes=[
            pltpu.VMEM((bands, tiles + 4, parts, planes, LANES), bf16),
            pltpu.VMEM((bands, 4 * tiles, LANES), bf16),
            pltpu.VMEM((bands, 4 * tiles, LANES), bf16),
            pltpu.VMEM((bands, 4 * tiles, LANES), bf16),
            pltpu.VMEM((bands, 4 * tiles, LANES), bf16),
            pltpu.VMEM((2, 16 * tiles, LANES), f32),
            pltpu.VMEM((16 * ROWS_PER_STEP, LANES), f32),
            pltpu.VMEM((3, 6 * LANES, 2 * LANES), bf16),
            pltpu.VMEM((tiles, 16, LANES), bf16),
            pltpu.VMEM((half, 16, LANES), bf16),
            pltpu.VMEM((half, 16, LANES), bf16),
            pltpu.VMEM((half, 16, LANES), bf16),
            pltpu.VMEM((relayed, piece, 16, LANES), bf16),
            pltpu.VMEM((tiles, 16, LANES), bf16),
            pltpu.VMEM((tiles, 4, 8, LANES), f32),
            dma((bands, 4)),
            dma((2, 4)),
            dma((copies,)),
            dma((copies,)),
            dma((copies,)),
            dma((copies,)),
            dma,
            dma,
            dma((DENSITY_PIECES,)),
            dma((DENSITY_PIECES,)),
            dma((relayed,)),
            dma((relayed,)),
            dma((DENSITY_PIECES,)),
            dma((DENSITY_PIECES,)),
        ],
        compiler_params=pltpu.CompilerParams(
            collective_id=0, has_side_effects=True, vmem_limit_bytes=48 << 20
        ),
    )(kpt_mult, occupied, view, core, local)
    written = pl.pallas_call(
        functools.partial(write_kernel, bands),
        out_shape=jax.ShapeDtypeStruct((bands, parts, tiles, planes, LANES), bf16),
        in_specs=[in_vmem],
        out_specs=anywhere,
        scratch_shapes=[dma((bands, 4))],
        compiler_params=pltpu.CompilerParams(vmem_limit_bytes=4 << 20),
    )(pltpu.with_memory_space_constraint(applied, pltpu.VMEM))
    return written.transpose(0, 1, 3, 2, 4).reshape(bands, parts, planes, cells)


def solution(mesh):
    placed = (P("ka", None, "brick", None), P("ka"), P("ka"), P("brick", None), P("brick", None))
    return jax.shard_map(
        shards, mesh=mesh, in_specs=placed, out_specs=P("ka", None, "brick", None), check_vma=False
    )
```

```python
import functools
import math

import jax
import jax.numpy as jnp
from jax import lax
from jax.experimental import pallas as pl
from jax.experimental.pallas import tpu as pltpu
from jax.sharding import PartitionSpec as P

NY = 192
FLOOR_FRACTION = 0.05
MESH = pl.DeviceIdType.MESH
LANES = 128
ROWS_PER_STEP = 16
LAST_PIECES = 4
DENSITY_PIECES = 4
MIX_STEP = 8
SUM_STEP = 6
POTENTIAL_STEP = 6
EARLY = 2


def cube_root(x):
    root = jnp.exp(jnp.log(jnp.abs(x)) * (1.0 / 3.0))
    return jnp.where(x == 0.0, 0.0, jnp.where(x < 0.0, -root, root))


def halo_kernel(
    bands,
    tiles,
    kpt_ref,
    occ_ref,
    x_hbm,
    core_ref,
    local_ref,
    out_ref,
    xb,
    send_up,
    send_down,
    from_below,
    from_above,
    partial_,
    stage,
    stencil,
    normal,
    own_density,
    partner_half,
    chip_half,
    opposite_half,
    relay,
    total_density,
    potential,
    load_sem,
    wrap_sem,
    up_send,
    up_recv,
    down_send,
    down_recv,
    pair_send,
    pair_recv,
    cross_send,
    cross_recv,
    relay_recv,
    relay_send,
    gather_send,
    gather_recv,
):
    ka, brick = lax.axis_index("ka"), lax.axis_index("brick")
    bricks = lax.axis_size("brick")
    groups = lax.axis_size("ka")
    side = lax.rem(ka, 2)
    has_above, has_below = brick < bricks - 1, brick > 0
    above = (ka, jnp.minimum(brick + 1, bricks - 1))
    below = (ka, jnp.maximum(brick - 1, 0))
    partner = (ka + 1 - 2 * side, brick)
    far = lax.rem(ka + 2, groups)
    opposite = (far, brick)
    mate = brick + 1 - 2 * lax.rem(brick, 2)
    row = lax.rem(brick, 4)
    edge = jnp.logical_or(row == 0, row == 3)
    inner = jnp.logical_not(edge)
    half = tiles // 2
    piece = half // DENSITY_PIECES
    direct = DENSITY_PIECES // 2

    barrier = pltpu.get_barrier_semaphore()

    @pl.when(has_above)
    def _():
        pl.semaphore_signal(barrier, inc=1, device_id=above, device_id_type=MESH)

    @pl.when(has_below)
    def _():
        pl.semaphore_signal(barrier, inc=1, device_id=below, device_id_type=MESH)

    for other in (partner, opposite, (far, mate)):
        pl.semaphore_signal(barrier, inc=1, device_id=other, device_id_type=MESH)

    def load(b, c):
        return pltpu.make_async_copy(
            x_hbm.at[b, c], xb.at[b, pl.ds(2, tiles), pl.ds(4 * c, 4)], load_sem.at[b, c]
        )

    def wrap(end, c):
        source = tiles - 2 if end == 0 else 0
        target = 0 if end == 0 else tiles + 2
        return pltpu.make_async_copy(
            x_hbm.at[:, c, pl.ds(source, 2)],
            xb.at[:, pl.ds(target, 2), pl.ds(4 * c, 4)],
            wrap_sem.at[end, c],
        )

    for b in range(bands):
        for c in range(4):
            load(b, c).start()
    for end in range(2):
        for c in range(4):
            wrap(end, c).start()

    last = bands - 1
    rows = 4 * tiles
    last_rows = rows // LAST_PIECES

    def slots(b):
        if b < last:
            return [(b, pl.ds(0, rows), b)]
        return [(b, pl.ds(k * last_rows, last_rows), last + k) for k in range(LAST_PIECES)]

    def up_copy(slot):
        b, r, s = slot
        return pltpu.make_async_remote_copy(
            send_up.at[b, r], from_below.at[b, r], up_send.at[s], up_recv.at[s],
            device_id=above, device_id_type=MESH,
        )

    def down_copy(slot):
        b, r, s = slot
        return pltpu.make_async_remote_copy(
            send_down.at[b, r], from_above.at[b, r], down_send.at[s], down_recv.at[s],
            device_id=below, device_id_type=MESH,
        )

    def extract(b):
        for c in range(4):
            load(b, c).wait()
        n = ROWS_PER_STEP

        def step(i, carry):
            j = i * n
            values = xb[b, pl.ds(2 + j, n)].reshape(n * 16, LANES)
            stage[...] = values.astype(jnp.float32)
            r = pl.multiple_of(4 * j, 4 * n)
            send_up[b, pl.ds(r, 4 * n)] = stage[pl.ds(3, 4 * n, stride=4)].astype(jnp.bfloat16)
            send_down[b, pl.ds(r, 4 * n)] = stage[pl.ds(0, 4 * n, stride=4)].astype(jnp.bfloat16)
            return carry

        lax.fori_loop(0, tiles // n, step, 0)

    def send(b):
        for slot in slots(b):

            @pl.when(has_above)
            def _():
                up_copy(slot).start()

            @pl.when(has_below)
            def _():
                down_copy(slot).start()

    for b in range(bands):
        extract(b)

    def weights_of(t):
        i = lax.broadcasted_iota(jnp.int32, (6 * LANES, 2 * LANES), 0) + 2 * LANES * (t - 1)
        o = lax.broadcasted_iota(jnp.int32, (6 * LANES, 2 * LANES), 1) + 2 * LANES * t
        diff = i - o
        y = o - jnp.where(o >= NY, NY, 0) - jnp.where(o >= 2 * NY, NY, 0) - jnp.where(o >= 3 * NY, NY, 0)
        forward = jnp.where(y == NY - 1, 1 - NY, 1)
        backward = jnp.where(y == 0, NY - 1, -1)
        near = jnp.where(diff == forward, -0.5, 0.0) + jnp.where(diff == backward, -0.5, 0.0)
        across = jnp.where(diff == NY, -0.5, 0.0) + jnp.where(diff == -NY, -0.5, 0.0)
        return (near + across + jnp.where(diff == 0, 3.0, 0.0)).astype(jnp.bfloat16)

    for t in range(3):
        stencil[t] = weights_of(t)
    size = LANES
    p = lax.broadcasted_iota(jnp.int32, (size, size), 0)
    q = lax.broadcasted_iota(jnp.int32, (size, size), 1)
    plane = lax.rem(p, 4)
    under = jnp.where(plane == 0, 0.0, jnp.where(p - q == 1, -0.5, 0.0))
    over = jnp.where(plane == 3, 0.0, jnp.where(q - p == 1, -0.5, 0.0))
    normal[...] = (under + over).astype(jnp.bfloat16)

    pl.semaphore_wait(
        barrier, 3 + has_above.astype(jnp.int32) + has_below.astype(jnp.int32)
    )
    for b in range(EARLY):
        send(b)

    low = lax.broadcasted_iota(jnp.int32, (8, LANES), 0) < 4
    weights = [
        (kpt_ref[b] * occ_ref[b]).astype(jnp.float32) * (1.0 / (2.0 * bands * groups))
        for b in range(bands)
    ]

    def swap(v):
        return pltpu.roll(v, 4, 0)

    def density_step(j, carry):
        for q in range(2):
            jj = 2 * j + q
            a = bb = cc = dd = None
            for b in range(bands):
                t = xb[b, 2 + jj].astype(jnp.float32)
                u, w = t[:8], t[8:]
                uw, ww = u * weights[b], w * weights[b]
                terms = (uw * u, ww * w, uw * w, uw * swap(w))
                if b == 0:
                    a, bb, cc, dd = terms
                else:
                    a, bb, cc, dd = (x + y for x, y in zip((a, bb, cc, dd), terms))
            n, z = a + bb, a - bb
            dd = jnp.where(low, dd, -dd)
            n, z = n + swap(n), z + swap(z)
            mx, my = 2.0 * (cc + swap(cc)), 2.0 * (dd + swap(dd))
            first = jnp.where(low, n, mx)
            second = jnp.where(low, my, z)
            own_density[jj] = jnp.concatenate([first, second], axis=0).astype(jnp.bfloat16)
        return carry

    mine, theirs = half * side, half * (1 - side)
    lax.fori_loop(
        0, half // 2, lambda i, c: density_step(theirs // 2 + i, c), 0
    )
    pair = pltpu.make_async_remote_copy(
        own_density.at[pl.ds(theirs, half)], partner_half, pair_send, pair_recv,
        device_id=partner, device_id_type=MESH,
    )
    lax.fori_loop(0, half // 16, lambda i, c: density_step(mine // 2 + i, c), 0)
    pair.start()
    lax.fori_loop(half // 16, half // 2, lambda i, c: density_step(mine // 2 + i, c), 0)

    pair.wait()

    def cross_copy(k):
        return pltpu.make_async_remote_copy(
            chip_half.at[pl.ds(k * piece, piece)], opposite_half.at[pl.ds(k * piece, piece)],
            cross_send.at[k], cross_recv.at[k], device_id=opposite, device_id_type=MESH,
        )

    def first_leg(k):
        return pltpu.make_async_remote_copy(
            chip_half.at[pl.ds(k * piece, piece)], relay.at[k - direct],
            cross_send.at[k], relay_recv.at[k - direct],
            device_id=(ka, mate), device_id_type=MESH,
        )

    def second_leg(k):
        return pltpu.make_async_remote_copy(
            relay.at[k - direct], opposite_half.at[pl.ds(k * piece, piece)],
            relay_send.at[k - direct], cross_recv.at[k],
            device_id=(far, mate), device_id_type=MESH,
        )

    def sum_half(i, carry):
        r = pl.ds(SUM_STEP * i, SUM_STEP)
        a = own_density[pl.ds(mine + SUM_STEP * i, SUM_STEP)].astype(jnp.float32)
        chip_half[r] = (a + partner_half[r].astype(jnp.float32)).astype(jnp.bfloat16)
        return carry

    def cross_start(k):
        if k < direct:
            cross_copy(k).start()
        else:

            @pl.when(edge)
            def _():
                first_leg(k).start()

            @pl.when(inner)
            def _():
                cross_copy(k).start()

    order = list(range(direct, DENSITY_PIECES)) + list(range(direct))
    for n, k in enumerate(order):
        lax.fori_loop(k * piece // SUM_STEP, (k + 1) * piece // SUM_STEP, sum_half, 0)
        if n:
            cross_start(order[n - 1])
    send(EARLY)
    cross_start(order[-1])
    for b in range(EARLY + 1, bands):
        send(b)

    for end in range(2):
        for c in range(4):
            wrap(end, c).wait()

    @pl.when(jnp.logical_not(has_below))
    def _():
        from_below[...] = jnp.zeros_like(from_below)

    @pl.when(jnp.logical_not(has_above))
    def _():
        from_above[...] = jnp.zeros_like(from_above)

    group = 8

    def kinetic(b):
        view = partial_.at[b]

        def step(i, carry):
            j0 = i * (6 * group)
            values = xb[b, pl.ds(j0, 6 * group + 4)]

            def block(first, count):
                return jnp.concatenate(
                    [
                        jnp.concatenate([values[6 * g + first + q] for g in range(group)], axis=0)
                        for q in range(count)
                    ],
                    axis=1,
                )

            for t in range(3):
                product = jnp.dot(
                    block(2 * t, 6), stencil[t], preferred_element_type=jnp.float32
                ) + jnp.dot(
                    normal[...], block(2 * t + 2, 2), preferred_element_type=jnp.float32
                )
                for g in range(group):
                    for e in range(2):
                        s = pl.multiple_of(16 * (j0 + 6 * g + 2 * t + e), 16)
                        view[pl.ds(s, 16)] = product[
                            16 * g : 16 * g + 16, LANES * e : LANES * (e + 1)
                        ]
            return carry

        lax.fori_loop(0, tiles // (6 * group), step, 0)

    kinetic(0)
    for k in range(direct, DENSITY_PIECES):
        kinetic(k - direct + 1)

        @pl.when(inner)
        def _():
            first_leg(k).wait_recv()
            second_leg(k).start()

    for b in range(DENSITY_PIECES - direct + 1, bands):
        kinetic(b)

    def sum_total(i, carry):
        r = pl.ds(SUM_STEP * i, SUM_STEP)
        a = chip_half[r].astype(jnp.float32) + opposite_half[r].astype(jnp.float32)
        total_density[pl.ds(mine + SUM_STEP * i, SUM_STEP)] = a.astype(jnp.bfloat16)
        return carry

    def gather(k):
        r = pl.ds(mine + k * piece, piece)
        return pltpu.make_async_remote_copy(
            total_density.at[r], total_density.at[r], gather_send.at[k], gather_recv.at[k],
            device_id=partner, device_id_type=MESH,
        )

    order = list(range(DENSITY_PIECES))
    for k in order:
        cross_copy(k).wait_recv()
        lax.fori_loop(k * piece // SUM_STEP, (k + 1) * piece // SUM_STEP, sum_total, 0)
        if k:
            gather(k - 1).start()

    def potential_of(j):
        t = total_density[j].astype(jnp.float32)
        first, second = t[:8], t[8:]
        other_first, other_second = swap(first), swap(second)
        n = jnp.where(low, first, other_first)
        mx = jnp.where(low, other_first, first)
        my = jnp.where(low, second, other_second)
        z = jnp.where(low, other_second, second)
        core = core_ref[j]
        local = local_ref[j]
        electrons = n + jnp.concatenate([core, core], axis=0)
        magnitude = jnp.sqrt(mx * mx + my * my + z * z)
        upper = -cube_root(3.0 / math.pi * (electrons + magnitude))
        lower = -cube_root(3.0 / math.pi * (electrons - magnitude))
        factor = 0.5 * (upper - lower) / jnp.maximum(magnitude, FLOOR_FRACTION * electrons)
        v = 0.5 * (upper + lower) + jnp.concatenate([local, local], axis=0)
        bz, by = factor * z, factor * my
        potential[j, 0] = v + bz
        potential[j, 1] = v - bz
        potential[j, 2] = factor * mx
        potential[j, 3] = jnp.where(low, by, -by)

    def potential_range(start, count):
        def step(i, carry):
            for q in range(POTENTIAL_STEP):
                potential_of(start + POTENTIAL_STEP * i + q)
            return carry

        lax.fori_loop(0, count // POTENTIAL_STEP, step, 0)

    potential_range(mine, (DENSITY_PIECES - 1) * piece)
    gather(DENSITY_PIECES - 1).start()
    potential_range(mine + (DENSITY_PIECES - 1) * piece, piece)

    def gathered(k):
        r = pl.ds(theirs + k * piece, piece)
        return pltpu.make_async_remote_copy(
            total_density.at[r], total_density.at[r], gather_send.at[k], gather_recv.at[k],
            device_id=partner, device_id_type=MESH,
        )

    for k in range(DENSITY_PIECES):
        gathered(k).wait_recv()
        potential_range(theirs + k * piece, piece)

    def mix(b):
        view = partial_.at[b]

        def step(i, carry):
            for q in range(MIX_STEP):
                j = i * MIX_STEP + q
                x = xb[b, j + 2].astype(jnp.float32)
                u, w = x[:8], x[8:]
                s = pl.multiple_of(16 * j, 16)
                bx, by = potential[j, 2], potential[j, 3]
                hu = view[pl.ds(s, 8)] + potential[j, 0] * u + bx * w + by * swap(w)
                hw = view[pl.ds(s + 8, 8)] + potential[j, 1] * w + bx * u - by * swap(u)
                view[pl.ds(s, 8)] = hu
                view[pl.ds(s + 8, 8)] = hw
            return carry

        lax.fori_loop(0, tiles // MIX_STEP, step, 0)

    def finish(b):
        n = ROWS_PER_STEP

        def step(i, carry):
            r = pl.multiple_of(4 * n * i, 4 * n)
            s = pl.multiple_of(16 * n * i, 16 * n)
            below_values = from_below[b, pl.ds(r, 4 * n)].astype(jnp.float32)
            above_values = from_above[b, pl.ds(r, 4 * n)].astype(jnp.float32)
            lows, highs = pl.ds(s, 4 * n, stride=4), pl.ds(s + 3, 4 * n, stride=4)
            view = partial_.at[b]
            view[lows] = view[lows] - 0.5 * below_values
            view[highs] = view[highs] - 0.5 * above_values
            done = view[pl.ds(s, 16 * n)].astype(jnp.bfloat16)
            out_ref[b, pl.ds(n * i, n)] = done.reshape(n, 16, LANES)
            return carry

        per_slot = tiles // n // len(slots(b))
        rest = tiles // n - per_slot * len(slots(b))
        start = 0
        for m, slot in enumerate(slots(b)):

            @pl.when(has_below)
            def _():
                up_copy(slot).wait_recv()

            @pl.when(has_above)
            def _():
                down_copy(slot).wait_recv()

            stop = ((m + 1) * tiles // len(slots(b))) // n
            lax.fori_loop(start, stop, step, 0)
            start = stop

    for b in range(bands):
        mix(b)
    for b in range(last):
        finish(b)

    pair_done = []
    for k in range(DENSITY_PIECES):
        cross_copy(k).wait_send()
        gather(k).wait_send()
    for k in range(direct, DENSITY_PIECES):

        @pl.when(inner)
        def _():
            second_leg(k).wait_send()

    for b in range(bands):
        for slot in slots(b):

            @pl.when(has_above)
            def _():
                up_copy(slot).wait_send()

            @pl.when(has_below)
            def _():
                down_copy(slot).wait_send()

    finish(last)


def write_kernel(bands, in_ref, out_hbm, sem):
    copies = [
        pltpu.make_async_copy(in_ref.at[b, :, pl.ds(4 * c, 4)], out_hbm.at[b, c], sem.at[b, c])
        for b in range(bands)
        for c in range(4)
    ]
    for copy in copies:
        copy.start()
    for copy in copies:
        copy.wait()


def shards(spinors, kpt_mult, occupied, core_density, local_potential):
    bands, parts, planes, cells = spinors.shape
    tiles = cells // LANES
    half = tiles // 2
    piece = half // DENSITY_PIECES
    relayed = DENSITY_PIECES - DENSITY_PIECES // 2
    copies = bands - 1 + LAST_PIECES
    bf16, f32 = jnp.bfloat16, jnp.float32
    view = spinors.reshape(bands, parts, planes, tiles, LANES).transpose(0, 1, 3, 2, 4)
    core = core_density.reshape(planes, tiles, LANES).transpose(1, 0, 2)
    local = local_potential.reshape(planes, tiles, LANES).transpose(1, 0, 2)
    dma = pltpu.SemaphoreType.DMA
    in_vmem = pl.BlockSpec(memory_space=pltpu.VMEM)
    in_smem = pl.BlockSpec(memory_space=pltpu.SMEM)
    anywhere = pl.BlockSpec(memory_space=pl.ANY)
    applied = pl.pallas_call(
        functools.partial(halo_kernel, bands, tiles),
        out_shape=pltpu.VMEM((bands, tiles, parts * planes, LANES), bf16),
        in_specs=[in_smem, in_smem, anywhere, in_vmem, in_vmem],
        out_specs=in_vmem,
        scratch_shapes=[
            pltpu.VMEM((bands, tiles + 4, parts * planes, LANES), bf16),
            pltpu.VMEM((bands, 4 * tiles, LANES), bf16),
            pltpu.VMEM((bands, 4 * tiles, LANES), bf16),
            pltpu.VMEM((bands, 4 * tiles, LANES), bf16),
            pltpu.VMEM((bands, 4 * tiles, LANES), bf16),
            pltpu.VMEM((bands, 16 * tiles, LANES), f32),
            pltpu.VMEM((16 * ROWS_PER_STEP, LANES), f32),
            pltpu.VMEM((3, 6 * LANES, 2 * LANES), bf16),
            pltpu.VMEM((LANES, LANES), bf16),
            pltpu.VMEM((tiles, 16, LANES), bf16),
            pltpu.VMEM((half, 16, LANES), bf16),
            pltpu.VMEM((half, 16, LANES), bf16),
            pltpu.VMEM((half, 16, LANES), bf16),
            pltpu.VMEM((relayed, piece, 16, LANES), bf16),
            pltpu.VMEM((tiles, 16, LANES), bf16),
            pltpu.VMEM((tiles, 4, 8, LANES), f32),
            dma((bands, 4)),
            dma((2, 4)),
            dma((copies,)),
            dma((copies,)),
            dma((copies,)),
            dma((copies,)),
            dma,
            dma,
            dma((DENSITY_PIECES,)),
            dma((DENSITY_PIECES,)),
            dma((relayed,)),
            dma((relayed,)),
            dma((DENSITY_PIECES,)),
            dma((DENSITY_PIECES,)),
        ],
        compiler_params=pltpu.CompilerParams(
            collective_id=0, has_side_effects=True, vmem_limit_bytes=54 << 20
        ),
    )(kpt_mult, occupied, view, core, local)
    written = pl.pallas_call(
        functools.partial(write_kernel, bands),
        out_shape=jax.ShapeDtypeStruct((bands, parts, tiles, planes, LANES), bf16),
        in_specs=[in_vmem],
        out_specs=anywhere,
        scratch_shapes=[dma((bands, 4))],
        compiler_params=pltpu.CompilerParams(vmem_limit_bytes=4 << 20),
    )(pltpu.with_memory_space_constraint(applied, pltpu.VMEM))
    return written.transpose(0, 1, 3, 2, 4).reshape(bands, parts, planes, cells)


def solution(mesh):
    placed = (P("ka", None, "brick", None), P("ka"), P("ka"), P("brick", None), P("brick", None))
    return jax.shard_map(
        shards, mesh=mesh, in_specs=placed, out_specs=P("ka", None, "brick", None), check_vma=False
    )
```

```python
import functools
import math

import jax
import jax.numpy as jnp
from jax import lax
from jax.experimental import pallas as pl
from jax.experimental.pallas import tpu as pltpu
from jax.sharding import PartitionSpec as P

NY = 192
FLOOR_FRACTION = 0.05
MESH = pl.DeviceIdType.MESH
LANES = 128
ROWS_PER_STEP = 16
LAST_PIECES = 4
DENSITY_PIECES = 4
MIX_STEP = 8
SUM_STEP = 6
POTENTIAL_STEP = 6
EARLY = 2


def cube_root(x):
    root = jnp.exp(jnp.log(jnp.abs(x)) * (1.0 / 3.0))
    return jnp.where(x == 0.0, 0.0, jnp.where(x < 0.0, -root, root))


def halo_kernel(
    bands,
    tiles,
    kpt_hbm,
    occ_hbm,
    x_hbm,
    core_hbm,
    local_hbm,
    out_ref,
    kpt_ref,
    occ_ref,
    core_ref,
    local_ref,
    xb,
    send_up,
    send_down,
    from_below,
    from_above,
    partial_,
    stage,
    stencil,
    normal,
    own_density,
    partner_half,
    chip_half,
    opposite_half,
    relay,
    total_density,
    potential,
    load_sem,
    wrap_sem,
    field_sem,
    up_send,
    up_recv,
    down_send,
    down_recv,
    pair_send,
    pair_recv,
    cross_send,
    cross_recv,
    relay_recv,
    relay_send,
    gather_send,
    gather_recv,
):
    ka, brick = lax.axis_index("ka"), lax.axis_index("brick")
    bricks = lax.axis_size("brick")
    groups = lax.axis_size("ka")
    side = lax.rem(ka, 2)
    has_above, has_below = brick < bricks - 1, brick > 0
    above = (ka, jnp.minimum(brick + 1, bricks - 1))
    below = (ka, jnp.maximum(brick - 1, 0))
    partner = (ka + 1 - 2 * side, brick)
    far = lax.rem(ka + 2, groups)
    opposite = (far, brick)
    mate = brick + 1 - 2 * lax.rem(brick, 2)
    row = lax.rem(brick, 4)
    edge = jnp.logical_or(row == 0, row == 3)
    inner = jnp.logical_not(edge)
    half = tiles // 2
    piece = half // DENSITY_PIECES
    direct = DENSITY_PIECES // 2

    barrier = pltpu.get_barrier_semaphore()

    @pl.when(has_above)
    def _():
        pl.semaphore_signal(barrier, inc=1, device_id=above, device_id_type=MESH)

    @pl.when(has_below)
    def _():
        pl.semaphore_signal(barrier, inc=1, device_id=below, device_id_type=MESH)

    for other in (partner, opposite, (far, mate)):
        pl.semaphore_signal(barrier, inc=1, device_id=other, device_id_type=MESH)

    def load(b, c):
        return pltpu.make_async_copy(
            x_hbm.at[b, c], xb.at[b, pl.ds(2, tiles), pl.ds(4 * c, 4)], load_sem.at[b, c]
        )

    def wrap(end, c):
        source = tiles - 2 if end == 0 else 0
        target = 0 if end == 0 else tiles + 2
        return pltpu.make_async_copy(
            x_hbm.at[:, c, pl.ds(source, 2)],
            xb.at[:, pl.ds(target, 2), pl.ds(4 * c, 4)],
            wrap_sem.at[end, c],
        )

    for b in range(bands):
        for c in range(4):
            load(b, c).start()
    for end in range(2):
        for c in range(4):
            wrap(end, c).start()
    fields = [
        pltpu.make_async_copy(source, target, field_sem.at[k])
        for k, (source, target) in enumerate(
            ((kpt_hbm, kpt_ref), (occ_hbm, occ_ref), (core_hbm, core_ref), (local_hbm, local_ref))
        )
    ]
    for field in fields:
        field.start()

    def weights_of(t):
        i = lax.broadcasted_iota(jnp.int32, (6 * LANES, 2 * LANES), 0) + 2 * LANES * (t - 1)
        o = lax.broadcasted_iota(jnp.int32, (6 * LANES, 2 * LANES), 1) + 2 * LANES * t
        diff = i - o
        y = o - jnp.where(o >= NY, NY, 0) - jnp.where(o >= 2 * NY, NY, 0) - jnp.where(o >= 3 * NY, NY, 0)
        forward = jnp.where(y == NY - 1, 1 - NY, 1)
        backward = jnp.where(y == 0, NY - 1, -1)
        near = jnp.where(diff == forward, -0.5, 0.0) + jnp.where(diff == backward, -0.5, 0.0)
        across = jnp.where(diff == NY, -0.5, 0.0) + jnp.where(diff == -NY, -0.5, 0.0)
        return (near + across + jnp.where(diff == 0, 3.0, 0.0)).astype(jnp.bfloat16)

    for t in range(3):
        stencil[t] = weights_of(t)
    size = LANES
    p = lax.broadcasted_iota(jnp.int32, (size, size), 0)
    q = lax.broadcasted_iota(jnp.int32, (size, size), 1)
    plane = lax.rem(p, 4)
    under = jnp.where(plane == 0, 0.0, jnp.where(p - q == 1, -0.5, 0.0))
    over = jnp.where(plane == 3, 0.0, jnp.where(q - p == 1, -0.5, 0.0))
    normal[...] = (under + over).astype(jnp.bfloat16)

    last = bands - 1
    rows = 4 * tiles
    last_rows = rows // LAST_PIECES

    def slots(b):
        if b < last:
            return [(b, pl.ds(0, rows), b)]
        return [(b, pl.ds(k * last_rows, last_rows), last + k) for k in range(LAST_PIECES)]

    def up_copy(slot):
        b, r, s = slot
        return pltpu.make_async_remote_copy(
            send_up.at[b, r], from_below.at[b, r], up_send.at[s], up_recv.at[s],
            device_id=above, device_id_type=MESH,
        )

    def down_copy(slot):
        b, r, s = slot
        return pltpu.make_async_remote_copy(
            send_down.at[b, r], from_above.at[b, r], down_send.at[s], down_recv.at[s],
            device_id=below, device_id_type=MESH,
        )

    def extract(b):
        for c in range(4):
            load(b, c).wait()
        n = ROWS_PER_STEP

        def step(i, carry):
            j = i * n
            values = xb[b, pl.ds(2 + j, n)].reshape(n * 16, LANES)
            stage[...] = values.astype(jnp.float32)
            r = pl.multiple_of(4 * j, 4 * n)
            send_up[b, pl.ds(r, 4 * n)] = stage[pl.ds(3, 4 * n, stride=4)].astype(jnp.bfloat16)
            send_down[b, pl.ds(r, 4 * n)] = stage[pl.ds(0, 4 * n, stride=4)].astype(jnp.bfloat16)
            return carry

        lax.fori_loop(0, tiles // n, step, 0)

    def send(b):
        for slot in slots(b):

            @pl.when(has_above)
            def _():
                up_copy(slot).start()

            @pl.when(has_below)
            def _():
                down_copy(slot).start()

    for b in range(EARLY + 1):
        extract(b)

    pl.semaphore_wait(
        barrier, 3 + has_above.astype(jnp.int32) + has_below.astype(jnp.int32)
    )
    for b in range(EARLY):
        send(b)
    for b in range(EARLY + 1, bands):
        extract(b)

    for field in fields:
        field.wait()

    low = lax.broadcasted_iota(jnp.int32, (8, LANES), 0) < 4
    weights = [
        (kpt_ref[b] * occ_ref[b]).astype(jnp.float32) * (1.0 / (2.0 * bands * groups))
        for b in range(bands)
    ]

    def swap(v):
        return pltpu.roll(v, 4, 0)

    def density_step(j, carry):
        for q in range(2):
            jj = 2 * j + q
            a = bb = cc = dd = None
            for b in range(bands):
                t = xb[b, 2 + jj].astype(jnp.float32)
                u, w = t[:8], t[8:]
                uw, ww = u * weights[b], w * weights[b]
                terms = (uw * u, ww * w, uw * w, uw * swap(w))
                if b == 0:
                    a, bb, cc, dd = terms
                else:
                    a, bb, cc, dd = (x + y for x, y in zip((a, bb, cc, dd), terms))
            n, z = a + bb, a - bb
            dd = jnp.where(low, dd, -dd)
            n, z = n + swap(n), z + swap(z)
            mx, my = 2.0 * (cc + swap(cc)), 2.0 * (dd + swap(dd))
            first = jnp.where(low, n, mx)
            second = jnp.where(low, my, z)
            own_density[jj] = jnp.concatenate([first, second], axis=0).astype(jnp.bfloat16)
        return carry

    mine, theirs = half * side, half * (1 - side)
    lax.fori_loop(
        0, half // 2, lambda i, c: density_step(theirs // 2 + i, c), 0
    )
    pair = pltpu.make_async_remote_copy(
        own_density.at[pl.ds(theirs, half)], partner_half, pair_send, pair_recv,
        device_id=partner, device_id_type=MESH,
    )
    lax.fori_loop(0, half // 16, lambda i, c: density_step(mine // 2 + i, c), 0)
    pair.start()
    lax.fori_loop(half // 16, half // 2, lambda i, c: density_step(mine // 2 + i, c), 0)

    pair.wait()

    def cross_copy(k):
        return pltpu.make_async_remote_copy(
            chip_half.at[pl.ds(k * piece, piece)], opposite_half.at[pl.ds(k * piece, piece)],
            cross_send.at[k], cross_recv.at[k], device_id=opposite, device_id_type=MESH,
        )

    def first_leg(k):
        return pltpu.make_async_remote_copy(
            chip_half.at[pl.ds(k * piece, piece)], relay.at[k - direct],
            cross_send.at[k], relay_recv.at[k - direct],
            device_id=(ka, mate), device_id_type=MESH,
        )

    def second_leg(k):
        return pltpu.make_async_remote_copy(
            relay.at[k - direct], opposite_half.at[pl.ds(k * piece, piece)],
            relay_send.at[k - direct], cross_recv.at[k],
            device_id=(far, mate), device_id_type=MESH,
        )

    def sum_half(i, carry):
        r = pl.ds(SUM_STEP * i, SUM_STEP)
        a = own_density[pl.ds(mine + SUM_STEP * i, SUM_STEP)].astype(jnp.float32)
        chip_half[r] = (a + partner_half[r].astype(jnp.float32)).astype(jnp.bfloat16)
        return carry

    def cross_start(k):
        if k < direct:
            cross_copy(k).start()
        else:

            @pl.when(edge)
            def _():
                first_leg(k).start()

            @pl.when(inner)
            def _():
                cross_copy(k).start()

    order = list(range(direct, DENSITY_PIECES)) + list(range(direct))
    for n, k in enumerate(order):
        lax.fori_loop(k * piece // SUM_STEP, (k + 1) * piece // SUM_STEP, sum_half, 0)
        if n:
            cross_start(order[n - 1])
    send(EARLY)
    cross_start(order[-1])
    for b in range(EARLY + 1, bands):
        send(b)

    for end in range(2):
        for c in range(4):
            wrap(end, c).wait()

    @pl.when(jnp.logical_not(has_below))
    def _():
        from_below[...] = jnp.zeros_like(from_below)

    @pl.when(jnp.logical_not(has_above))
    def _():
        from_above[...] = jnp.zeros_like(from_above)

    group = 8

    def kinetic(b):
        view = partial_.at[b]

        def step(i, carry):
            j0 = i * (6 * group)
            values = xb[b, pl.ds(j0, 6 * group + 4)]

            def block(first, count):
                return jnp.concatenate(
                    [
                        jnp.concatenate([values[6 * g + first + q] for g in range(group)], axis=0)
                        for q in range(count)
                    ],
                    axis=1,
                )

            for t in range(3):
                product = jnp.dot(
                    block(2 * t, 6), stencil[t], preferred_element_type=jnp.float32
                ) + jnp.dot(
                    normal[...], block(2 * t + 2, 2), preferred_element_type=jnp.float32
                )
                for g in range(group):
                    for e in range(2):
                        s = pl.multiple_of(16 * (j0 + 6 * g + 2 * t + e), 16)
                        view[pl.ds(s, 16)] = product[
                            16 * g : 16 * g + 16, LANES * e : LANES * (e + 1)
                        ]
            return carry

        lax.fori_loop(0, tiles // (6 * group), step, 0)

    kinetic(0)
    for k in range(direct, DENSITY_PIECES):
        kinetic(k - direct + 1)

        @pl.when(inner)
        def _():
            first_leg(k).wait_recv()
            second_leg(k).start()

    for b in range(DENSITY_PIECES - direct + 1, bands):
        kinetic(b)

    def sum_total(i, carry):
        r = pl.ds(SUM_STEP * i, SUM_STEP)
        a = chip_half[r].astype(jnp.float32) + opposite_half[r].astype(jnp.float32)
        total_density[pl.ds(mine + SUM_STEP * i, SUM_STEP)] = a.astype(jnp.bfloat16)
        return carry

    def gather(k):
        r = pl.ds(mine + k * piece, piece)
        return pltpu.make_async_remote_copy(
            total_density.at[r], total_density.at[r], gather_send.at[k], gather_recv.at[k],
            device_id=partner, device_id_type=MESH,
        )

    order = list(range(DENSITY_PIECES))
    for k in order:
        cross_copy(k).wait_recv()
        lax.fori_loop(k * piece // SUM_STEP, (k + 1) * piece // SUM_STEP, sum_total, 0)
        if k:
            gather(k - 1).start()

    def potential_of(j):
        t = total_density[j].astype(jnp.float32)
        first, second = t[:8], t[8:]
        other_first, other_second = swap(first), swap(second)
        n = jnp.where(low, first, other_first)
        mx = jnp.where(low, other_first, first)
        my = jnp.where(low, second, other_second)
        z = jnp.where(low, other_second, second)
        core = core_ref[j]
        local = local_ref[j]
        electrons = n + jnp.concatenate([core, core], axis=0)
        magnitude = jnp.sqrt(mx * mx + my * my + z * z)
        upper = -cube_root(3.0 / math.pi * (electrons + magnitude))
        lower = -cube_root(3.0 / math.pi * (electrons - magnitude))
        factor = 0.5 * (upper - lower) / jnp.maximum(magnitude, FLOOR_FRACTION * electrons)
        v = 0.5 * (upper + lower) + jnp.concatenate([local, local], axis=0)
        bz, by = factor * z, factor * my
        potential[j, 0] = v + bz
        potential[j, 1] = v - bz
        potential[j, 2] = factor * mx
        potential[j, 3] = jnp.where(low, by, -by)

    def potential_range(start, count):
        def step(i, carry):
            for q in range(POTENTIAL_STEP):
                potential_of(start + POTENTIAL_STEP * i + q)
            return carry

        lax.fori_loop(0, count // POTENTIAL_STEP, step, 0)

    potential_range(mine, (DENSITY_PIECES - 1) * piece)
    gather(DENSITY_PIECES - 1).start()
    potential_range(mine + (DENSITY_PIECES - 1) * piece, piece)

    def gathered(k):
        r = pl.ds(theirs + k * piece, piece)
        return pltpu.make_async_remote_copy(
            total_density.at[r], total_density.at[r], gather_send.at[k], gather_recv.at[k],
            device_id=partner, device_id_type=MESH,
        )

    for k in range(DENSITY_PIECES):
        gathered(k).wait_recv()
        potential_range(theirs + k * piece, piece)

    def mix(b):
        view = partial_.at[b]

        def step(i, carry):
            for q in range(MIX_STEP):
                j = i * MIX_STEP + q
                x = xb[b, j + 2].astype(jnp.float32)
                u, w = x[:8], x[8:]
                s = pl.multiple_of(16 * j, 16)
                bx, by = potential[j, 2], potential[j, 3]
                hu = view[pl.ds(s, 8)] + potential[j, 0] * u + bx * w + by * swap(w)
                hw = view[pl.ds(s + 8, 8)] + potential[j, 1] * w + bx * u - by * swap(u)
                view[pl.ds(s, 8)] = hu
                view[pl.ds(s + 8, 8)] = hw
            return carry

        lax.fori_loop(0, tiles // MIX_STEP, step, 0)

    def finish(b):
        n = ROWS_PER_STEP

        def step(i, carry):
            r = pl.multiple_of(4 * n * i, 4 * n)
            s = pl.multiple_of(16 * n * i, 16 * n)
            below_values = from_below[b, pl.ds(r, 4 * n)].astype(jnp.float32)
            above_values = from_above[b, pl.ds(r, 4 * n)].astype(jnp.float32)
            lows, highs = pl.ds(s, 4 * n, stride=4), pl.ds(s + 3, 4 * n, stride=4)
            view = partial_.at[b]
            view[lows] = view[lows] - 0.5 * below_values
            view[highs] = view[highs] - 0.5 * above_values
            done = view[pl.ds(s, 16 * n)].astype(jnp.bfloat16)
            out_ref[b, pl.ds(n * i, n)] = done.reshape(n, 16, LANES)
            return carry

        per_slot = tiles // n // len(slots(b))
        rest = tiles // n - per_slot * len(slots(b))
        start = 0
        for m, slot in enumerate(slots(b)):

            @pl.when(has_below)
            def _():
                up_copy(slot).wait_recv()

            @pl.when(has_above)
            def _():
                down_copy(slot).wait_recv()

            stop = ((m + 1) * tiles // len(slots(b))) // n
            lax.fori_loop(start, stop, step, 0)
            start = stop

    for b in range(bands):
        mix(b)
    for b in range(last):
        finish(b)

    pair_done = []
    for k in range(DENSITY_PIECES):
        cross_copy(k).wait_send()
        gather(k).wait_send()
    for k in range(direct, DENSITY_PIECES):

        @pl.when(inner)
        def _():
            second_leg(k).wait_send()

    for b in range(bands):
        for slot in slots(b):

            @pl.when(has_above)
            def _():
                up_copy(slot).wait_send()

            @pl.when(has_below)
            def _():
                down_copy(slot).wait_send()

    finish(last)


def write_kernel(bands, in_ref, out_hbm, sem):
    copies = [
        pltpu.make_async_copy(in_ref.at[b, :, pl.ds(4 * c, 4)], out_hbm.at[b, c], sem.at[b, c])
        for b in range(bands)
        for c in range(4)
    ]
    for copy in copies:
        copy.start()
    for copy in copies:
        copy.wait()


def shards(spinors, kpt_mult, occupied, core_density, local_potential):
    bands, parts, planes, cells = spinors.shape
    tiles = cells // LANES
    half = tiles // 2
    piece = half // DENSITY_PIECES
    relayed = DENSITY_PIECES - DENSITY_PIECES // 2
    copies = bands - 1 + LAST_PIECES
    bf16, f32 = jnp.bfloat16, jnp.float32
    view = spinors.reshape(bands, parts, planes, tiles, LANES).transpose(0, 1, 3, 2, 4)
    core = core_density.reshape(planes, tiles, LANES).transpose(1, 0, 2)
    local = local_potential.reshape(planes, tiles, LANES).transpose(1, 0, 2)
    dma = pltpu.SemaphoreType.DMA
    in_vmem = pl.BlockSpec(memory_space=pltpu.VMEM)
    anywhere = pl.BlockSpec(memory_space=pl.ANY)
    applied = pl.pallas_call(
        functools.partial(halo_kernel, bands, tiles),
        out_shape=pltpu.VMEM((bands, tiles, parts * planes, LANES), bf16),
        in_specs=[anywhere] * 5,
        out_specs=in_vmem,
        scratch_shapes=[
            pltpu.SMEM((bands,), jnp.int32),
            pltpu.SMEM((bands,), jnp.int32),
            pltpu.VMEM((tiles, planes, LANES), f32),
            pltpu.VMEM((tiles, planes, LANES), f32),
            pltpu.VMEM((bands, tiles + 4, parts * planes, LANES), bf16),
            pltpu.VMEM((bands, 4 * tiles, LANES), bf16),
            pltpu.VMEM((bands, 4 * tiles, LANES), bf16),
            pltpu.VMEM((bands, 4 * tiles, LANES), bf16),
            pltpu.VMEM((bands, 4 * tiles, LANES), bf16),
            pltpu.VMEM((bands, 16 * tiles, LANES), f32),
            pltpu.VMEM((16 * ROWS_PER_STEP, LANES), f32),
            pltpu.VMEM((3, 6 * LANES, 2 * LANES), bf16),
            pltpu.VMEM((LANES, LANES), bf16),
            pltpu.VMEM((tiles, 16, LANES), bf16),
            pltpu.VMEM((half, 16, LANES), bf16),
            pltpu.VMEM((half, 16, LANES), bf16),
            pltpu.VMEM((half, 16, LANES), bf16),
            pltpu.VMEM((relayed, piece, 16, LANES), bf16),
            pltpu.VMEM((tiles, 16, LANES), bf16),
            pltpu.VMEM((tiles, 4, 8, LANES), f32),
            dma((bands, 4)),
            dma((2, 4)),
            dma((4,)),
            dma((copies,)),
            dma((copies,)),
            dma((copies,)),
            dma((copies,)),
            dma,
            dma,
            dma((DENSITY_PIECES,)),
            dma((DENSITY_PIECES,)),
            dma((relayed,)),
            dma((relayed,)),
            dma((DENSITY_PIECES,)),
            dma((DENSITY_PIECES,)),
        ],
        compiler_params=pltpu.CompilerParams(
            collective_id=0, has_side_effects=True, vmem_limit_bytes=54 << 20
        ),
    )(kpt_mult, occupied, view, core, local)
    written = pl.pallas_call(
        functools.partial(write_kernel, bands),
        out_shape=jax.ShapeDtypeStruct((bands, parts, tiles, planes, LANES), bf16),
        in_specs=[in_vmem],
        out_specs=anywhere,
        scratch_shapes=[dma((bands, 4))],
        compiler_params=pltpu.CompilerParams(vmem_limit_bytes=4 << 20),
    )(pltpu.with_memory_space_constraint(applied, pltpu.VMEM))
    return written.transpose(0, 1, 3, 2, 4).reshape(bands, parts, planes, cells)


def solution(mesh):
    placed = (P("ka", None, "brick", None), P("ka"), P("ka"), P("brick", None), P("brick", None))
    return jax.shard_map(
        shards, mesh=mesh, in_specs=placed, out_specs=P("ka", None, "brick", None), check_vma=False
    )
```

```python
import functools
import math

import jax
import jax.numpy as jnp
from jax import lax
from jax.experimental import pallas as pl
from jax.experimental.pallas import tpu as pltpu
from jax.sharding import PartitionSpec as P

NY = 192
FLOOR_FRACTION = 0.05
MESH = pl.DeviceIdType.MESH
LANES = 128
ROWS_PER_STEP = 16
LAST_PIECES = 4
DENSITY_PIECES = 4
MIX_STEP = 8
SUM_STEP = 6
POTENTIAL_STEP = 6
DIRECT_PIECES = 2
EARLY = 2


def cube_root(x):
    root = jnp.exp(jnp.log(jnp.abs(x)) * (1.0 / 3.0))
    return jnp.where(x == 0.0, 0.0, jnp.where(x < 0.0, -root, root))


def halo_kernel(
    bands,
    tiles,
    kpt_hbm,
    occ_hbm,
    x_hbm,
    core_hbm,
    local_hbm,
    out_ref,
    kpt_ref,
    occ_ref,
    core_ref,
    local_ref,
    xb,
    send_up,
    send_down,
    from_below,
    from_above,
    partial_,
    stage,
    stencil,
    normal,
    own_density,
    partner_half,
    chip_half,
    opposite_half,
    relay,
    total_density,
    potential,
    load_sem,
    wrap_sem,
    field_sem,
    up_send,
    up_recv,
    down_send,
    down_recv,
    pair_send,
    pair_recv,
    cross_send,
    cross_recv,
    relay_recv,
    relay_send,
    gather_send,
    gather_recv,
):
    ka, brick = lax.axis_index("ka"), lax.axis_index("brick")
    bricks = lax.axis_size("brick")
    groups = lax.axis_size("ka")
    side = lax.rem(ka, 2)
    has_above, has_below = brick < bricks - 1, brick > 0
    above = (ka, jnp.minimum(brick + 1, bricks - 1))
    below = (ka, jnp.maximum(brick - 1, 0))
    partner = (ka + 1 - 2 * side, brick)
    far = lax.rem(ka + 2, groups)
    opposite = (far, brick)
    mate = brick + 1 - 2 * lax.rem(brick, 2)
    row = lax.rem(brick, 4)
    edge = jnp.logical_or(row == 0, row == 3)
    inner = jnp.logical_not(edge)
    half = tiles // 2
    piece = half // DENSITY_PIECES
    direct = DIRECT_PIECES

    barrier = pltpu.get_barrier_semaphore()

    @pl.when(has_above)
    def _():
        pl.semaphore_signal(barrier, inc=1, device_id=above, device_id_type=MESH)

    @pl.when(has_below)
    def _():
        pl.semaphore_signal(barrier, inc=1, device_id=below, device_id_type=MESH)

    for other in (partner, opposite, (far, mate)):
        pl.semaphore_signal(barrier, inc=1, device_id=other, device_id_type=MESH)

    def load(b, c):
        return pltpu.make_async_copy(
            x_hbm.at[b, c], xb.at[b, pl.ds(2, tiles), pl.ds(4 * c, 4)], load_sem.at[b, c]
        )

    def wrap(end, c):
        source = tiles - 2 if end == 0 else 0
        target = 0 if end == 0 else tiles + 2
        return pltpu.make_async_copy(
            x_hbm.at[:, c, pl.ds(source, 2)],
            xb.at[:, pl.ds(target, 2), pl.ds(4 * c, 4)],
            wrap_sem.at[end, c],
        )

    for b in range(bands):
        for c in range(4):
            load(b, c).start()
    for end in range(2):
        for c in range(4):
            wrap(end, c).start()
    fields = [
        pltpu.make_async_copy(source, target, field_sem.at[k])
        for k, (source, target) in enumerate(
            ((kpt_hbm, kpt_ref), (occ_hbm, occ_ref), (core_hbm, core_ref), (local_hbm, local_ref))
        )
    ]
    for field in fields:
        field.start()

    def weights_of(t):
        i = lax.broadcasted_iota(jnp.int32, (6 * LANES, 2 * LANES), 0) + 2 * LANES * (t - 1)
        o = lax.broadcasted_iota(jnp.int32, (6 * LANES, 2 * LANES), 1) + 2 * LANES * t
        diff = i - o
        y = o - jnp.where(o >= NY, NY, 0) - jnp.where(o >= 2 * NY, NY, 0) - jnp.where(o >= 3 * NY, NY, 0)
        forward = jnp.where(y == NY - 1, 1 - NY, 1)
        backward = jnp.where(y == 0, NY - 1, -1)
        near = jnp.where(diff == forward, -0.5, 0.0) + jnp.where(diff == backward, -0.5, 0.0)
        across = jnp.where(diff == NY, -0.5, 0.0) + jnp.where(diff == -NY, -0.5, 0.0)
        return (near + across + jnp.where(diff == 0, 3.0, 0.0)).astype(jnp.bfloat16)

    for t in range(3):
        stencil[t] = weights_of(t)
    size = LANES
    p = lax.broadcasted_iota(jnp.int32, (size, size), 0)
    q = lax.broadcasted_iota(jnp.int32, (size, size), 1)
    plane = lax.rem(p, 4)
    under = jnp.where(plane == 0, 0.0, jnp.where(p - q == 1, -0.5, 0.0))
    over = jnp.where(plane == 3, 0.0, jnp.where(q - p == 1, -0.5, 0.0))
    normal[...] = (under + over).astype(jnp.bfloat16)

    last = bands - 1
    rows = 4 * tiles
    last_rows = rows // LAST_PIECES

    def slots(b):
        if b < last:
            return [(b, pl.ds(0, rows), b)]
        return [(b, pl.ds(k * last_rows, last_rows), last + k) for k in range(LAST_PIECES)]

    def up_copy(slot):
        b, r, s = slot
        return pltpu.make_async_remote_copy(
            send_up.at[b, r], from_below.at[b, r], up_send.at[s], up_recv.at[s],
            device_id=above, device_id_type=MESH,
        )

    def down_copy(slot):
        b, r, s = slot
        return pltpu.make_async_remote_copy(
            send_down.at[b, r], from_above.at[b, r], down_send.at[s], down_recv.at[s],
            device_id=below, device_id_type=MESH,
        )

    def extract(b):
        for c in range(4):
            load(b, c).wait()
        n = ROWS_PER_STEP

        def step(i, carry):
            j = i * n
            values = xb[b, pl.ds(2 + j, n)].reshape(n * 16, LANES)
            stage[...] = values.astype(jnp.float32)
            r = pl.multiple_of(4 * j, 4 * n)
            send_up[b, pl.ds(r, 4 * n)] = stage[pl.ds(3, 4 * n, stride=4)].astype(jnp.bfloat16)
            send_down[b, pl.ds(r, 4 * n)] = stage[pl.ds(0, 4 * n, stride=4)].astype(jnp.bfloat16)
            return carry

        lax.fori_loop(0, tiles // n, step, 0)

    def send(b):
        for slot in slots(b):

            @pl.when(has_above)
            def _():
                up_copy(slot).start()

            @pl.when(has_below)
            def _():
                down_copy(slot).start()

    for b in range(EARLY + 1):
        extract(b)

    pl.semaphore_wait(
        barrier, 3 + has_above.astype(jnp.int32) + has_below.astype(jnp.int32)
    )
    for b in range(EARLY):
        send(b)
    for b in range(EARLY + 1, bands):
        extract(b)

    for field in fields:
        field.wait()

    low = lax.broadcasted_iota(jnp.int32, (8, LANES), 0) < 4
    weights = [
        (kpt_ref[b] * occ_ref[b]).astype(jnp.float32) * (1.0 / (2.0 * bands * groups))
        for b in range(bands)
    ]

    def swap(v):
        return pltpu.roll(v, 4, 0)

    def density_step(j, carry):
        for q in range(2):
            jj = 2 * j + q
            a = bb = cc = dd = None
            for b in range(bands):
                t = xb[b, 2 + jj].astype(jnp.float32)
                u, w = t[:8], t[8:]
                uw, ww = u * weights[b], w * weights[b]
                terms = (uw * u, ww * w, uw * w, uw * swap(w))
                if b == 0:
                    a, bb, cc, dd = terms
                else:
                    a, bb, cc, dd = (x + y for x, y in zip((a, bb, cc, dd), terms))
            n, z = a + bb, a - bb
            dd = jnp.where(low, dd, -dd)
            n, z = n + swap(n), z + swap(z)
            mx, my = 2.0 * (cc + swap(cc)), 2.0 * (dd + swap(dd))
            first = jnp.where(low, n, mx)
            second = jnp.where(low, my, z)
            own_density[jj] = jnp.concatenate([first, second], axis=0).astype(jnp.bfloat16)
        return carry

    mine, theirs = half * side, half * (1 - side)
    lax.fori_loop(
        0, half // 2, lambda i, c: density_step(theirs // 2 + i, c), 0
    )
    pair = pltpu.make_async_remote_copy(
        own_density.at[pl.ds(theirs, half)], partner_half, pair_send, pair_recv,
        device_id=partner, device_id_type=MESH,
    )
    lax.fori_loop(0, half // 16, lambda i, c: density_step(mine // 2 + i, c), 0)
    pair.start()
    lax.fori_loop(half // 16, half // 2, lambda i, c: density_step(mine // 2 + i, c), 0)

    pair.wait()

    def cross_copy(k):
        return pltpu.make_async_remote_copy(
            chip_half.at[pl.ds(k * piece, piece)], opposite_half.at[pl.ds(k * piece, piece)],
            cross_send.at[k], cross_recv.at[k], device_id=opposite, device_id_type=MESH,
        )

    def first_leg(k):
        return pltpu.make_async_remote_copy(
            chip_half.at[pl.ds(k * piece, piece)], relay.at[k - direct],
            cross_send.at[k], relay_recv.at[k - direct],
            device_id=(ka, mate), device_id_type=MESH,
        )

    def second_leg(k):
        return pltpu.make_async_remote_copy(
            relay.at[k - direct], opposite_half.at[pl.ds(k * piece, piece)],
            relay_send.at[k - direct], cross_recv.at[k],
            device_id=(far, mate), device_id_type=MESH,
        )

    def sum_half(i, carry):
        r = pl.ds(SUM_STEP * i, SUM_STEP)
        a = own_density[pl.ds(mine + SUM_STEP * i, SUM_STEP)].astype(jnp.float32)
        chip_half[r] = (a + partner_half[r].astype(jnp.float32)).astype(jnp.bfloat16)
        return carry

    def cross_start(k):
        if k < direct:
            cross_copy(k).start()
        else:

            @pl.when(edge)
            def _():
                first_leg(k).start()

            @pl.when(inner)
            def _():
                cross_copy(k).start()

    group = 8

    def kinetic(b):
        view = partial_.at[b]

        def step(i, carry):
            j0 = i * (6 * group)
            values = xb[b, pl.ds(j0, 6 * group + 4)]

            def block(first, count):
                return jnp.concatenate(
                    [
                        jnp.concatenate([values[6 * g + first + q] for g in range(group)], axis=0)
                        for q in range(count)
                    ],
                    axis=1,
                )

            for t in range(3):
                product = jnp.dot(
                    block(2 * t, 6), stencil[t], preferred_element_type=jnp.float32
                ) + jnp.dot(
                    normal[...], block(2 * t + 2, 2), preferred_element_type=jnp.float32
                )
                for g in range(group):
                    for e in range(2):
                        s = pl.multiple_of(16 * (j0 + 6 * g + 2 * t + e), 16)
                        view[pl.ds(s, 16)] = product[
                            16 * g : 16 * g + 16, LANES * e : LANES * (e + 1)
                        ]
            return carry

        lax.fori_loop(0, tiles // (6 * group), step, 0)

    for end in range(2):
        for c in range(4):
            wrap(end, c).wait()

    order = list(range(direct, DENSITY_PIECES)) + list(range(direct))
    for n, k in enumerate(order):
        lax.fori_loop(k * piece // SUM_STEP, (k + 1) * piece // SUM_STEP, sum_half, 0)
        if n:
            cross_start(order[n - 1])
    send(EARLY)
    kinetic(0)
    cross_start(order[-1])
    for b in range(EARLY + 1, bands):
        send(b)

    @pl.when(jnp.logical_not(has_below))
    def _():
        from_below[...] = jnp.zeros_like(from_below)

    @pl.when(jnp.logical_not(has_above))
    def _():
        from_above[...] = jnp.zeros_like(from_above)

    for k in range(direct, DENSITY_PIECES):
        kinetic(k - direct + 1)

        @pl.when(inner)
        def _():
            first_leg(k).wait_recv()
            second_leg(k).start()

    for b in range(DENSITY_PIECES - direct + 1, bands):
        kinetic(b)

    def sum_total(i, carry):
        r = pl.ds(SUM_STEP * i, SUM_STEP)
        a = chip_half[r].astype(jnp.float32) + opposite_half[r].astype(jnp.float32)
        total_density[pl.ds(mine + SUM_STEP * i, SUM_STEP)] = a.astype(jnp.bfloat16)
        return carry

    def gather(k):
        r = pl.ds(mine + k * piece, piece)
        return pltpu.make_async_remote_copy(
            total_density.at[r], total_density.at[r], gather_send.at[k], gather_recv.at[k],
            device_id=partner, device_id_type=MESH,
        )

    order = list(range(DENSITY_PIECES))
    for k in order:
        cross_copy(k).wait_recv()
        lax.fori_loop(k * piece // SUM_STEP, (k + 1) * piece // SUM_STEP, sum_total, 0)
        if k:
            gather(k - 1).start()

    def potential_of(j):
        t = total_density[j].astype(jnp.float32)
        first, second = t[:8], t[8:]
        other_first, other_second = swap(first), swap(second)
        n = jnp.where(low, first, other_first)
        mx = jnp.where(low, other_first, first)
        my = jnp.where(low, second, other_second)
        z = jnp.where(low, other_second, second)
        core = core_ref[j]
        local = local_ref[j]
        electrons = n + jnp.concatenate([core, core], axis=0)
        magnitude = jnp.sqrt(mx * mx + my * my + z * z)
        upper = -cube_root(3.0 / math.pi * (electrons + magnitude))
        lower = -cube_root(3.0 / math.pi * (electrons - magnitude))
        factor = 0.5 * (upper - lower) / jnp.maximum(magnitude, FLOOR_FRACTION * electrons)
        v = 0.5 * (upper + lower) + jnp.concatenate([local, local], axis=0)
        bz, by = factor * z, factor * my
        potential[j, 0] = v + bz
        potential[j, 1] = v - bz
        potential[j, 2] = factor * mx
        potential[j, 3] = jnp.where(low, by, -by)

    def potential_range(start, count):
        def step(i, carry):
            for q in range(POTENTIAL_STEP):
                potential_of(start + POTENTIAL_STEP * i + q)
            return carry

        lax.fori_loop(0, count // POTENTIAL_STEP, step, 0)

    potential_range(mine, (DENSITY_PIECES - 1) * piece)
    gather(DENSITY_PIECES - 1).start()
    potential_range(mine + (DENSITY_PIECES - 1) * piece, piece)

    def gathered(k):
        r = pl.ds(theirs + k * piece, piece)
        return pltpu.make_async_remote_copy(
            total_density.at[r], total_density.at[r], gather_send.at[k], gather_recv.at[k],
            device_id=partner, device_id_type=MESH,
        )

    for k in range(DENSITY_PIECES):
        gathered(k).wait_recv()
        potential_range(theirs + k * piece, piece)

    def mix(b):
        view = partial_.at[b]

        def step(i, carry):
            for q in range(MIX_STEP):
                j = i * MIX_STEP + q
                x = xb[b, j + 2].astype(jnp.float32)
                u, w = x[:8], x[8:]
                s = pl.multiple_of(16 * j, 16)
                bx, by = potential[j, 2], potential[j, 3]
                hu = view[pl.ds(s, 8)] + potential[j, 0] * u + bx * w + by * swap(w)
                hw = view[pl.ds(s + 8, 8)] + potential[j, 1] * w + bx * u - by * swap(u)
                view[pl.ds(s, 8)] = hu
                view[pl.ds(s + 8, 8)] = hw
            return carry

        lax.fori_loop(0, tiles // MIX_STEP, step, 0)

    def finish(b):
        n = ROWS_PER_STEP

        def step(i, carry):
            r = pl.multiple_of(4 * n * i, 4 * n)
            s = pl.multiple_of(16 * n * i, 16 * n)
            below_values = from_below[b, pl.ds(r, 4 * n)].astype(jnp.float32)
            above_values = from_above[b, pl.ds(r, 4 * n)].astype(jnp.float32)
            lows, highs = pl.ds(s, 4 * n, stride=4), pl.ds(s + 3, 4 * n, stride=4)
            view = partial_.at[b]
            view[lows] = view[lows] - 0.5 * below_values
            view[highs] = view[highs] - 0.5 * above_values
            done = view[pl.ds(s, 16 * n)].astype(jnp.bfloat16)
            out_ref[b, pl.ds(n * i, n)] = done.reshape(n, 16, LANES)
            return carry

        per_slot = tiles // n // len(slots(b))
        rest = tiles // n - per_slot * len(slots(b))
        start = 0
        for m, slot in enumerate(slots(b)):

            @pl.when(has_below)
            def _():
                up_copy(slot).wait_recv()

            @pl.when(has_above)
            def _():
                down_copy(slot).wait_recv()

            stop = ((m + 1) * tiles // len(slots(b))) // n
            lax.fori_loop(start, stop, step, 0)
            start = stop

    for b in range(bands):
        mix(b)
    for b in range(last):
        finish(b)

    pair_done = []
    for k in range(DENSITY_PIECES):
        cross_copy(k).wait_send()
        gather(k).wait_send()
    for k in range(direct, DENSITY_PIECES):

        @pl.when(inner)
        def _():
            second_leg(k).wait_send()

    for b in range(bands):
        for slot in slots(b):

            @pl.when(has_above)
            def _():
                up_copy(slot).wait_send()

            @pl.when(has_below)
            def _():
                down_copy(slot).wait_send()

    finish(last)


def write_kernel(bands, in_ref, out_hbm, sem):
    copies = [
        pltpu.make_async_copy(in_ref.at[b, :, pl.ds(4 * c, 4)], out_hbm.at[b, c], sem.at[b, c])
        for b in range(bands)
        for c in range(4)
    ]
    for copy in copies:
        copy.start()
    for copy in copies:
        copy.wait()


def shards(spinors, kpt_mult, occupied, core_density, local_potential):
    bands, parts, planes, cells = spinors.shape
    tiles = cells // LANES
    half = tiles // 2
    piece = half // DENSITY_PIECES
    relayed = DENSITY_PIECES - DIRECT_PIECES
    copies = bands - 1 + LAST_PIECES
    bf16, f32 = jnp.bfloat16, jnp.float32
    view = spinors.reshape(bands, parts, planes, tiles, LANES).transpose(0, 1, 3, 2, 4)
    core = core_density.reshape(planes, tiles, LANES).transpose(1, 0, 2)
    local = local_potential.reshape(planes, tiles, LANES).transpose(1, 0, 2)
    dma = pltpu.SemaphoreType.DMA
    in_vmem = pl.BlockSpec(memory_space=pltpu.VMEM)
    anywhere = pl.BlockSpec(memory_space=pl.ANY)
    applied = pl.pallas_call(
        functools.partial(halo_kernel, bands, tiles),
        out_shape=pltpu.VMEM((bands, tiles, parts * planes, LANES), bf16),
        in_specs=[anywhere] * 5,
        out_specs=in_vmem,
        scratch_shapes=[
            pltpu.SMEM((bands,), jnp.int32),
            pltpu.SMEM((bands,), jnp.int32),
            pltpu.VMEM((tiles, planes, LANES), f32),
            pltpu.VMEM((tiles, planes, LANES), f32),
            pltpu.VMEM((bands, tiles + 4, parts * planes, LANES), bf16),
            pltpu.VMEM((bands, 4 * tiles, LANES), bf16),
            pltpu.VMEM((bands, 4 * tiles, LANES), bf16),
            pltpu.VMEM((bands, 4 * tiles, LANES), bf16),
            pltpu.VMEM((bands, 4 * tiles, LANES), bf16),
            pltpu.VMEM((bands, 16 * tiles, LANES), f32),
            pltpu.VMEM((16 * ROWS_PER_STEP, LANES), f32),
            pltpu.VMEM((3, 6 * LANES, 2 * LANES), bf16),
            pltpu.VMEM((LANES, LANES), bf16),
            pltpu.VMEM((tiles, 16, LANES), bf16),
            pltpu.VMEM((half, 16, LANES), bf16),
            pltpu.VMEM((half, 16, LANES), bf16),
            pltpu.VMEM((half, 16, LANES), bf16),
            pltpu.VMEM((relayed, piece, 16, LANES), bf16),
            pltpu.VMEM((tiles, 16, LANES), bf16),
            pltpu.VMEM((tiles, 4, 8, LANES), f32),
            dma((bands, 4)),
            dma((2, 4)),
            dma((4,)),
            dma((copies,)),
            dma((copies,)),
            dma((copies,)),
            dma((copies,)),
            dma,
            dma,
            dma((DENSITY_PIECES,)),
            dma((DENSITY_PIECES,)),
            dma((relayed,)),
            dma((relayed,)),
            dma((DENSITY_PIECES,)),
            dma((DENSITY_PIECES,)),
        ],
        compiler_params=pltpu.CompilerParams(
            collective_id=0, has_side_effects=True, vmem_limit_bytes=54 << 20
        ),
    )(kpt_mult, occupied, view, core, local)
    written = pl.pallas_call(
        functools.partial(write_kernel, bands),
        out_shape=jax.ShapeDtypeStruct((bands, parts, tiles, planes, LANES), bf16),
        in_specs=[in_vmem],
        out_specs=anywhere,
        scratch_shapes=[dma((bands, 4))],
        compiler_params=pltpu.CompilerParams(vmem_limit_bytes=4 << 20),
    )(pltpu.with_memory_space_constraint(applied, pltpu.VMEM))
    return written.transpose(0, 1, 3, 2, 4).reshape(bands, parts, planes, cells)


def solution(mesh):
    placed = (P("ka", None, "brick", None), P("ka"), P("ka"), P("brick", None), P("brick", None))
    return jax.shard_map(
        shards, mesh=mesh, in_specs=placed, out_specs=P("ka", None, "brick", None), check_vma=False
    )
```
